512 devices in a mesh: segment: 2 (over x_lo), seq: 32 (over z, core), tensor: 8 (over y, x_hi).
Axes of the slice: x: 4 (x_hi: 2, x_lo: 2; x = x_hi * 2 + x_lo), y: 4, z: 16, core: 2. Of those that a mesh axis runs over, the one named last changes fastest.
Arguments:
- vision_states: bfloat16 [6144, 7680], P(('segment', 'seq'), 'tensor'), may hold values from -6 to 6
- kv_weight: bfloat16 [7680, 2048], P('tensor'), may hold values from -0.09375 to 0.09375
- key_gain: float32 [128], replicated, may hold values from 0.5 to 1.5
- queries: bfloat16 [16384, 8, 1024], P('seq', 'tensor', 'segment'), may hold values from -700 to 700
- tile_tokens: int32 [4], replicated, may hold values from 768 to 1536, as said below
- text_tiles: int32 [16384, 2], P('seq'), may hold values from 0 to 4, as said below
Outputs:
- attended: bfloat16 [16384, 8, 1024], P('seq', 'tensor', 'segment')
The draws below stay inside these ranges and needn't reach their ends.
Inputs may be any that keep to these rules, and one draw needn't show every extreme that they name: The valid tokens of tile i are its first tile_tokens[i] positions of 1536; some tile is full. Text token r sees tiles text_tiles[r, 0] to text_tiles[r, 1] - 1, with text_tiles[r, 0] <= text_tiles[r, 1]; an empty range means it sees no image.
All inputs are finite; a program needn't handle non-finite values.
Results may differ from the reference program's by a relative error of at most 0.012.
The reference program's roundings to bfloat16 on the way (of `keys`, `values` and `weights`) count: a program that leaves them out, or rounds other values in their place, can miss the bound.
Values may be sent and summed in bfloat16 or wider, within the bound.
A program may use at most 64 MiB of HBM per device.

```python
import math
import jax
import jax.numpy as jnp
from jax import lax

DV = 7680
KVH = 8
HD = 128
TILES = 4
VT = 6144
TT = 16384
TILE_LEN = 1536
GROUP = 8


def draw_queries(key, part):
    first_key = jax.random.fold_in(key, 0)
    shape = (TT, KVH, GROUP * HD)
    base = jax.random.normal(first_key, shape, jnp.float32) * 2.5
    return jnp.clip(base, -15.0, 15.0).astype(jnp.bfloat16)


def draw_tile_tokens(key, part):
    first_key, second_key = jax.random.split(key)
    counts = jax.random.randint(first_key, (TILES,), TILE_LEN // 2, TILE_LEN + 1, dtype=jnp.int32)
    full_tile = jax.random.randint(second_key, (), 0, TILES, dtype=jnp.int32)
    return jnp.where(jnp.arange(TILES, dtype=jnp.int32) == full_tile, TILE_LEN, counts).astype(jnp.int32)


def draw_text_tiles(key, part):
    first_key, second_key, third_key = jax.random.split(key, 3)
    lower = jax.random.randint(first_key, (TT,), 0, TILES, dtype=jnp.int32)
    upper = jax.random.randint(second_key, (TT,), lower + 1, TILES + 1, dtype=jnp.int32)
    unseen = jax.random.randint(third_key, (TT,), 0, 8, dtype=jnp.int32) == 0
    upper = jnp.where(unseen, lower, upper)
    return jnp.stack([lower, upper], axis=1).astype(jnp.int32)


def spiked(values, stream_key, source, target, blocks, factor):
    def block_of(axis_at):
        return (jnp.arange(values.shape[axis_at]) // (values.shape[axis_at] // blocks)).reshape((-1,) + (1,) * (values.ndim - 1 - axis_at))

    one_side = jax.random.permutation(stream_key, blocks)[block_of(target)]
    far = (block_of(target) + blocks // 2) % blocks
    return jnp.where((block_of(source) == one_side) | (block_of(source) == far), factor * values, values)


def steps_of(key, extent, cuts, low, high):
    loudness = 1.0
    for position, blocks in cuts:
        steps = jax.random.uniform(jax.random.fold_in(jax.random.fold_in(key, 6), position), (blocks,), jnp.float32, low / len(cuts), high / len(cuts))
        loudness = loudness * jnp.repeat(jnp.exp(steps), extent[position] // blocks).reshape((-1,) + (1,) * (len(extent) - 1 - position))
    return loudness


def scatter_about(rng, shape, spread, reach, pieces=(), kind=jnp.bfloat16):
    entries = jax.random.normal(rng, shape, jnp.float32) * spread
    if len(pieces) > 0:
        entries = steps_of(rng, shape, pieces, -0.22, 0.18) * entries
    return jnp.clip(entries, min=-reach, max=reach).astype(kind)


def gaussian_with(own_key, dims, scale, bound, cuts, heavy, kind=jnp.bfloat16):
    drawn = scale * jax.random.normal(own_key, dims, jnp.float32)
    if cuts:
        drawn = drawn * steps_of(own_key, dims, cuts, -0.22, 0.18)
    return jnp.clip(spiked(drawn, jax.random.fold_in(own_key, 3), *heavy), -bound, bound).astype(kind)


def setup_inputs(seed: int = 0) -> dict:
    seeds = jax.random.split(jax.random.key(seed), 7)
    vision_states = scatter_about(seeds[0], (VT, DV), 1.0, 6.0, ((0, 64), (1, 8)))
    kv_weight = gaussian_with(seeds[1], (DV, KVH * 2 * HD), DV ** -0.5, 0.09375, ((0, 8),), (0, 1, 8, 2.0))
    key_gain = jnp.clip(jax.random.uniform(seeds[2], (HD,), jnp.float32, 0.5, 1.5), 0.5, 1.5)
    queries = draw_queries(jax.random.fold_in(seeds[6], 71), 0)
    tile_tokens = draw_tile_tokens(jax.random.fold_in(seeds[6], 71), 0)
    text_tiles = draw_text_tiles(jax.random.fold_in(seeds[6], 71), 0)
    return dict(vision_states=vision_states, kv_weight=kv_weight, key_gain=key_gain, queries=queries, tile_tokens=tile_tokens, text_tiles=text_tiles)


def reference(vision_states, kv_weight, key_gain, queries, tile_tokens, text_tiles):
    projected = jnp.dot(vision_states, kv_weight, preferred_element_type=jnp.float32)
    projected = projected.reshape(VT, KVH, 2 * HD)
    keys_raw = projected[:, :, :HD]
    mean_sq = lax.optimization_barrier(jnp.mean(keys_raw * keys_raw, axis=-1, keepdims=True))
    keys = (keys_raw * lax.rsqrt(mean_sq + 1e-05) * key_gain).astype(jnp.bfloat16)
    values = projected[:, :, HD:].astype(jnp.bfloat16)
    positions = jnp.arange(VT, dtype=jnp.int32)
    tile_ids = positions // TILE_LEN
    key_valid = positions % TILE_LEN < tile_tokens[tile_ids]
    score_scale = HD ** (-0.5)
    block_rows = math.gcd(TT, 512)
    query_blocks = queries.reshape(TT // block_rows, block_rows, KVH, GROUP, HD)
    lower_blocks = text_tiles[:, 0].reshape(TT // block_rows, block_rows)
    upper_blocks = text_tiles[:, 1].reshape(TT // block_rows, block_rows)
    keys_heads = jnp.transpose(keys, (1, 0, 2))
    values_heads = jnp.transpose(values, (1, 0, 2))

    def one_block(packed):
        query_block, lower, upper = packed
        visible = key_valid[None, :] & (tile_ids[None, :] >= lower[:, None]) & (tile_ids[None, :] < upper[:, None])
        unseen = (upper <= lower).astype(jnp.float32)

        def one_head(head_pack):
            query_head, key_head, value_head = head_pack
            scores = jnp.einsum('rgd,nd->rgn', query_head.astype(jnp.float32), key_head.astype(jnp.float32)) * score_scale
            key_mask = visible[:, None, :]
            masked = jnp.where(key_mask, scores, -1e+30)
            row_max = lax.optimization_barrier(jnp.max(masked, axis=-1, keepdims=True))
            expterm = jnp.where(key_mask, jnp.exp(masked - row_max), 0.0)
            denominator = lax.optimization_barrier(jnp.sum(expterm, axis=-1))
            weights = expterm.astype(jnp.bfloat16)
            numerator = jnp.einsum('rgn,nd->rgd', weights.astype(jnp.float32), value_head.astype(jnp.float32))
            return numerator / (denominator + unseen[:, None])[:, :, None]
        query_heads = jnp.transpose(query_block, (1, 0, 2, 3))
        outputs = lax.map(one_head, (query_heads, keys_heads, values_heads))
        return jnp.transpose(outputs, (1, 0, 2, 3)).reshape(block_rows, KVH, GROUP * HD)
    result = lax.map(one_block, (query_blocks, lower_blocks, upper_blocks))
    return result.reshape(TT, KVH, GROUP * HD).astype(jnp.bfloat16)
```

```python
import functools
import math

import jax
import jax.numpy as jnp
from jax import lax
from jax.experimental import pallas as pl
from jax.experimental.pallas import tpu as pltpu
from jax.sharding import PartitionSpec as P

MESH = pl.DeviceIdType.MESH
F32 = jnp.float32
BF16 = jnp.bfloat16
NEG = -1e30
SUB = 32
RING = 32
ORDER = ((0, 1), (0, 2), (1, 2), (1, 3), (0, 3), (0, 4), (1, 4), (2, 4), (2, 3), (3, 4))


def project_gather(
    nz, vis_ref, w_ref, gain_ref, q_ref, tt_ref,
    kv_ref, qs_ref, pt_ref, lohi_ref, flag_ref,
    w_buf, part_out, part_in, w_sem, rs_send, rs_recv,
    a_send, a_recv, b_send, b_recv, x_send, x_recv, n_send, n_recv, ca_send, ca_recv, cn_send, cn_recv,
):
    heads = w_buf.shape[0]
    hd = gain_ref.shape[1]
    width = 2 * hd
    rows = vis_ref.shape[0]
    seg = lax.axis_index("segment")
    seq = lax.axis_index("seq")
    ten = lax.axis_index("tensor")
    z, core = seq // 2, seq % 2
    up, down = (z + 1) % nz, (z + nz - 1) % nz
    to_up = {"seq": up * 2 + core}
    to_down = {"seq": down * 2 + core}
    to_x = {"segment": 1 - seg}
    to_core = {"seq": z * 2 + (1 - core)}

    def weight_copy(k):
        head = (ten + k) % heads
        cols = pl.ds(pl.multiple_of(head * width, width), width)
        return pltpu.make_async_copy(w_ref.at[:, cols], w_buf.at[k], w_sem.at[k])

    order = list(range(1, heads)) + [0]
    for k in order:
        weight_copy(k).start()

    barrier = pltpu.get_barrier_semaphore()
    for k in range(1, heads):
        pl.semaphore_signal(barrier, inc=1, device_id={"tensor": (ten + k) % heads}, device_id_type=MESH)
    for target in (to_up, to_down, to_x, to_core):
        pl.semaphore_signal(barrier, inc=1, device_id=target, device_id_type=MESH)
    pl.semaphore_wait(barrier, heads + 3)

    def partial_copy(k):
        return pltpu.make_async_remote_copy(
            src_ref=part_out.at[k], dst_ref=part_in.at[k], send_sem=rs_send.at[k], recv_sem=rs_recv.at[k],
            device_id={"tensor": (ten + k) % heads}, device_id_type=MESH,
        )

    for k in order:
        weight_copy(k).wait()
        part_out[k] = jnp.dot(vis_ref[...], w_buf[k], preferred_element_type=F32)
        if k:
            partial_copy(k).start()

    count = tt_ref.shape[1]
    low_row = tt_ref[0:1, :].astype(F32)
    high_row = tt_ref[1:2, :].astype(F32)
    rank_row = jnp.full_like(low_row, float(len(ORDER)))
    for place, (first, last) in enumerate(ORDER):
        rank_row = jnp.where((low_row == first) & (high_row == last), float(place), rank_row)
    row_id = lax.broadcasted_iota(jnp.int32, (count, count), 0)
    col_id = lax.broadcasted_iota(jnp.int32, (count, count), 1)
    here = row_id == col_id

    def column(row):
        return jnp.sum(jnp.where(here, row, 0.0), axis=1, keepdims=True)

    key_row = rank_row
    key_col = column(rank_row)
    ahead_row = (key_col < key_row) | ((key_col == key_row) & (row_id < col_id))
    place_row = jnp.sum(jnp.where(ahead_row, 1.0, 0.0), axis=0, keepdims=True)
    ahead_col = (key_row < key_col) | ((key_row == key_col) & (col_id < row_id))
    place_col = jnp.sum(jnp.where(ahead_col, 1.0, 0.0), axis=1, keepdims=True)
    perm = row_id.astype(F32) == place_row
    pt_ref[...] = jnp.where(col_id.astype(F32) == place_col, 1.0, 0.0).astype(BF16)
    qs_ref[...] = jnp.dot(
        jnp.where(perm, 1.0, 0.0).astype(BF16), q_ref[...], preferred_element_type=F32
    ).astype(BF16)
    low_sorted = jnp.sum(jnp.where(perm, low_row, 0.0), axis=1, keepdims=True)
    high_sorted = jnp.sum(jnp.where(perm, high_row, 0.0), axis=1, keepdims=True)
    lane = lax.broadcasted_iota(jnp.int32, (count, 128), 1)
    lohi_ref[...] = jnp.where(lane == 0, low_sorted, high_sorted)
    lane_f = lane.astype(F32)
    sees = jnp.where((low_sorted <= lane_f) & (lane_f < high_sorted), 1.0, 0.0)
    for block in range(count // SUB):
        flag_ref[block : block + 1, :] = jnp.max(
            sees[block * SUB : (block + 1) * SUB], axis=0, keepdims=True
        ).astype(jnp.int32)

    total = part_out[0]
    for k in range(1, heads):
        partial_copy(k).wait_recv()
        total = total + part_in[k]
    keys_raw = total[:, :hd]
    mean_sq = jnp.mean(keys_raw * keys_raw, axis=-1, keepdims=True)
    normed = keys_raw * lax.rsqrt(mean_sq + 1e-05) * gain_ref[...]

    def slot(segment, zz, cc):
        return segment * (2 * nz) + zz * 2 + cc

    mine = slot(seg, z, core)
    kv_ref[mine, :, :hd] = normed.astype(BF16)
    kv_ref[mine, :, hd:] = total[:, hd:].astype(BF16)

    def move(block, first, size, send, recv, target):
        piece = kv_ref.at[block, pl.ds(first, size)]
        return pltpu.make_async_remote_copy(
            src_ref=piece, dst_ref=piece, send_sem=send, recv_sem=recv, device_id=target, device_id_type=MESH
        )

    def ring_a(way, d, target):
        zz = (z + nz - d) % nz if way == 0 else (z + d) % nz
        return move(slot(seg, zz, core), 0, rows, a_send.at[way, d], a_recv.at[way, d], target)

    def ring_b(way, d, target):
        zz = (z + nz - d) % nz if way == 0 else (z + d) % nz
        return move(slot(1 - seg, zz, core), 0, RING, b_send.at[way, d], b_recv.at[way, d], target)

    def send_a(way, d):
        zz = (z + nz - d) % nz if way == 0 else (z + d) % nz
        return move(
            slot(seg, zz, core), 0, rows, a_send.at[way, d], a_recv.at[way, d + 1], to_up if way == 0 else to_down
        )

    def send_b(way, d):
        zz = (z + nz - d) % nz if way == 0 else (z + d) % nz
        return move(
            slot(1 - seg, zz, core), 0, RING, b_send.at[way, d], b_recv.at[way, d + 1], to_up if way == 0 else to_down
        )

    def x_copy(zz, mine_side):
        side = seg if mine_side else 1 - seg
        off = (zz + nz - z) % nz
        return move(slot(side, zz, core), RING, rows - RING, x_send.at[off], x_recv.at[off], to_x)

    def nb_copy(mine_side):
        side = seg if mine_side else 1 - seg
        return move(slot(side, z, core), 0, RING, n_send, n_recv, to_x)

    def core_copy(zz, own_column, outgoing):
        side = seg if own_column else 1 - seg
        off = (zz + nz - z) % nz
        send, recv = (ca_send, ca_recv) if own_column else (cn_send, cn_recv)
        cc = core if outgoing else 1 - core
        return move(slot(side, zz, cc), 0, rows, send.at[off], recv.at[off], to_core)

    half = nz // 2

    nb_copy(True).start()
    send_a(0, 0).start()
    send_a(1, 0).start()
    x_copy(z, True).start()
    nb_copy(False).wait_recv()
    send_b(0, 0).start()
    send_b(1, 0).start()
    core_copy(z, True, True).start()

    def hop(d, carry):
        above = (z + nz - d) % nz
        below = (z + d) % nz
        ring_a(0, d, to_up).wait_recv()
        send_a(0, d).start()
        ring_a(1, d, to_down).wait_recv()

        @pl.when(d < half - 1)
        def _():
            send_a(1, d).start()

        x_copy(above, True).start()
        x_copy(below, True).start()
        ring_b(0, d, to_up).wait_recv()

        @pl.when(d < half - 1)
        def _():
            send_b(0, d).start()

        ring_b(1, d, to_down).wait_recv()
        send_b(1, d).start()
        core_copy(above, True, True).start()
        core_copy(below, True, True).start()
        last = (z + nz - d + 1) % nz
        x_copy(last, False).wait_recv()
        core_copy(last, False, True).start()

        @pl.when(d > 1)
        def _():
            other = (z + d - 1) % nz
            x_copy(other, False).wait_recv()
            core_copy(other, False, True).start()

        return carry

    lax.fori_loop(1, half, hop, 0)
    far = (z + half) % nz
    ring_a(0, half, to_up).wait_recv()
    x_copy(far, True).start()
    core_copy(far, True, True).start()
    ring_b(1, half, to_down).wait_recv()
    for zz in ((z + half + 1) % nz, (z + half - 1) % nz, far):
        x_copy(zz, False).wait_recv()
        core_copy(zz, False, True).start()

    def finish(off, carry):
        zz = (z + off) % nz
        core_copy(zz, True, False).wait_recv()
        core_copy(zz, False, False).wait_recv()
        core_copy(zz, True, True).wait_send()
        core_copy(zz, False, True).wait_send()
        x_copy(zz, True).wait_send()
        return carry

    lax.fori_loop(0, nz, finish, 0)
    nb_copy(True).wait_send()
    for k in range(1, heads):
        partial_copy(k).wait_send()

    def finish_ring(d, carry):
        send_a(0, d).wait_send()
        send_b(1, d).wait_send()

        @pl.when(d < half - 1)
        def _():
            send_a(1, d).wait_send()
            send_b(0, d).wait_send()

        return carry

    lax.fori_loop(0, half, finish_ring, 0)


def attend(
    scale, tile_len, least, tokens_ref, flag_ref, kv_ref, qs_ref, pt_ref, lohi_ref, out_ref,
    acc, top, low_sum, sorted_out, blocks_of, *, group=2,
):
    tiles = kv_ref.shape[0] // tile_len
    hd = kv_ref.shape[1] // 2
    count = qs_ref.shape[0] // SUB
    heads = qs_ref.shape[1] // hd
    chunk = 256
    acc[...] = jnp.zeros_like(acc)
    low_sum[...] = jnp.zeros_like(low_sum)
    top[...] = jnp.full_like(top, NEG)
    factor = scale * math.log2(math.e)

    def visit(tile, n_chunks, masked, picked, valid):
        rows_of = []
        for block in picked:
            src = pl.multiple_of(jnp.where(block == count, 0, block) * SUB, SUB)
            for h in range(heads):
                rows_of.append(qs_ref[pl.ds(src, SUB), h * hd : (h + 1) * hd])
        q = jnp.concatenate(rows_of, axis=0)
        scores = []
        for c in range(n_chunks):
            at = pl.multiple_of(tile * tile_len + c * chunk, chunk)
            s = lax.dot_general(
                q, kv_ref[pl.ds(at, chunk), :hd], (((1,), (1,)), ((), ())), preferred_element_type=F32
            )
            if masked and c == n_chunks - 1:
                lane = lax.broadcasted_iota(jnp.int32, s.shape, 1)
                s = jnp.where(lane < valid - c * chunk, s, NEG)
            scores.append(s)
        best = scores[0]
        for s in scores[1:]:
            best = jnp.maximum(best, s)
        peak = jnp.max(best, axis=1, keepdims=True)
        part = None
        summed = None
        for c, s in enumerate(scores):
            at = pl.multiple_of(tile * tile_len + c * chunk, chunk)
            e = jnp.exp2((s - peak) * factor)
            part = e if part is None else part + e
            o = jnp.dot(e.astype(BF16), kv_ref[pl.ds(at, chunk), hd:], preferred_element_type=F32)
            summed = o if summed is None else summed + o
        row_sum = jnp.sum(part, axis=1, keepdims=True)
        span = heads * SUB
        for i, block in enumerate(picked):
            src = pl.multiple_of(jnp.where(block == count, 0, block) * SUB, SUB)
            low = lohi_ref[pl.ds(src, SUB), 0:1]
            high = lohi_ref[pl.ds(src, SUB), 1:2]
            tile_f = tile.astype(F32)
            seen = jnp.where((low <= tile_f) & (tile_f < high), 1.0, 0.0)
            seen = jnp.concatenate([seen] * heads, axis=0)
            part_slice = slice(i * span, (i + 1) * span)
            mine = jnp.where(seen > 0.0, peak[part_slice], NEG)
            old = top[block]
            new = jnp.maximum(old, mine)
            keep = jnp.exp2((old - new) * factor)
            take = jnp.where(seen > 0.0, jnp.exp2((mine - new) * factor), 0.0)
            top[block] = new
            low_sum[block] = low_sum[block] * keep + row_sum[part_slice] * take
            acc[block] = acc[block] * keep + summed[part_slice] * take

    def one_tile(tile, carry):
        def collect(block, found):
            blocks_of[found] = block
            return found + flag_ref[block, tile]

        found = lax.fori_loop(0, count, collect, 0)
        for i in range(group - 1):
            blocks_of[found + i] = count
        trips = (found + group - 1) // group
        valid = tokens_ref[tile]
        base = least // chunk
        extra = (valid - least + chunk - 1) // chunk
        for more in range((tile_len - least) // chunk + 1):

            @pl.when(extra == more)
            def _(more=more):
                def pair(i, c):
                    visit(tile, base + more, more > 0, [blocks_of[i * group + j] for j in range(group)], valid)
                    return c

                lax.fori_loop(0, trips, pair, 0)

        return carry

    lax.fori_loop(0, tiles, one_tile, 0)

    def close(block, carry):
        src = pl.multiple_of(block * SUB, SUB)
        low = lohi_ref[pl.ds(src, SUB), 0:1]
        high = lohi_ref[pl.ds(src, SUB), 1:2]
        unseen = jnp.where(high <= low, 1.0, 0.0)
        unseen = jnp.concatenate([unseen] * heads, axis=0)
        done = (acc[block] / (low_sum[block] + unseen)).astype(BF16)
        for h in range(heads):
            sorted_out[pl.ds(src, SUB), h * hd : (h + 1) * hd] = done[h * SUB : (h + 1) * SUB]
        return carry

    lax.fori_loop(0, count, close, 0)
    out_ref[...] = jnp.dot(pt_ref[...], sorted_out[...], preferred_element_type=F32).astype(BF16)


def run_attend(tile_tokens, flags, kv, qs, pt, lohi, head_dim):
    text_rows, cols = qs.shape
    tile_len = kv.shape[0] // tile_tokens.shape[0]
    span = (cols // head_dim) * SUB
    blocks = text_rows // SUB
    smem = pl.BlockSpec(memory_space=pltpu.SMEM)
    vmem = pl.BlockSpec(memory_space=pltpu.VMEM)
    return pl.pallas_call(
        functools.partial(attend, head_dim ** (-0.5), tile_len, tile_len // 2),
        out_shape=jax.ShapeDtypeStruct((text_rows, cols), BF16),
        in_specs=[smem, smem, vmem, vmem, vmem, vmem],
        out_specs=vmem,
        scratch_shapes=[
            pltpu.VMEM((blocks + 1, span, head_dim), F32),
            pltpu.VMEM((blocks + 1, span, head_dim), F32),
            pltpu.VMEM((blocks + 1, span, head_dim), F32),
            pltpu.VMEM((text_rows, cols), BF16),
            pltpu.SMEM((blocks + 8,), jnp.int32),
        ],
        compiler_params=pltpu.CompilerParams(vmem_limit_bytes=40 << 20),
        name="attend",
    )(tile_tokens, flags, kv, qs, pt, lohi)


def shards(vision_states, kv_weight, key_gain, queries, tile_tokens, text_tiles):
    head_dim = key_gain.shape[0]
    rows = vision_states.shape[0]
    heads = lax.axis_size("tensor")
    nz = lax.axis_size("seq") // 2
    pieces = lax.axis_size("segment") * lax.axis_size("seq")
    depth = vision_states.shape[1]
    text_rows = queries.shape[0]
    q = queries.reshape(text_rows, queries.shape[2])
    vmem = pl.BlockSpec(memory_space=pltpu.VMEM)
    dma = pltpu.SemaphoreType.DMA
    kv, qs, pt, lohi, flags = pl.pallas_call(
        functools.partial(project_gather, nz),
        out_shape=(
            jax.ShapeDtypeStruct((pieces, rows, 2 * head_dim), BF16),
            jax.ShapeDtypeStruct(q.shape, BF16),
            jax.ShapeDtypeStruct((text_rows, text_rows), BF16),
            jax.ShapeDtypeStruct((text_rows, 128), F32),
            jax.ShapeDtypeStruct((text_rows // SUB, 128), jnp.int32),
        ),
        in_specs=[vmem, pl.BlockSpec(memory_space=pl.ANY), vmem, vmem, vmem],
        out_specs=(vmem,) * 5,
        scratch_shapes=[
            pltpu.VMEM((heads, depth, 2 * head_dim), BF16),
            pltpu.VMEM((heads, rows, 2 * head_dim), F32),
            pltpu.VMEM((heads, rows, 2 * head_dim), F32),
            dma((heads,)), dma((heads,)), dma((heads,)),
            dma((2, nz // 2 + 1)), dma((2, nz // 2 + 1)), dma((2, nz // 2 + 1)), dma((2, nz // 2 + 1)),
            dma((nz,)), dma((nz,)), dma, dma,
            dma((nz,)), dma((nz,)), dma((nz,)), dma((nz,)),
        ],
        compiler_params=pltpu.CompilerParams(
            collective_id=0, has_side_effects=True, vmem_limit_bytes=40 << 20
        ),
        name="project_gather",
    )(vision_states, kv_weight, key_gain.reshape(1, head_dim), q, text_tiles.T)
    kv = kv.reshape(pieces * rows, 2 * head_dim)
    out = run_attend(tile_tokens, flags, kv, qs, pt, lohi, head_dim)
    return out.reshape(queries.shape)


def solution(mesh):
    placed = (
        P(("segment", "seq"), "tensor"),
        P("tensor", None),
        P(),
        P("seq", "tensor", "segment"),
        P(),
        P("seq", None),
    )
    return jax.shard_map(
        shards, mesh=mesh, in_specs=placed, out_specs=P("seq", "tensor", "segment"), check_vma=False
    )
```

```python
import functools
import math

import jax
import jax.numpy as jnp
from jax import lax
from jax.experimental import pallas as pl
from jax.experimental.pallas import tpu as pltpu
from jax.sharding import PartitionSpec as P

MESH = pl.DeviceIdType.MESH
F32 = jnp.float32
BF16 = jnp.bfloat16
NEG = -1e30
SUB = 16
TREE = {2: 0, 4: 2, 6: 4, 8: 6, 1: 0, 3: 2, 5: 4, 7: 6}
ARRIVAL = (2, 1, 4, 3, 6, 5, 8, 7)
LAG = 6
BLAG = 1
RING = 16
VALUE_PART = BF16
ORDER = ((0, 1), (0, 2), (1, 2), (1, 3), (0, 3), (0, 4), (1, 4), (2, 4), (2, 3), (3, 4))


def project_gather(
    nz, vis_hbm, w_hbm, gain_hbm, q_hbm, tt_hbm,
    kv_ref, qs_ref, pt_ref, lohi_ref, flag_ref,
    vis_ref, w_ref, gain_ref, q_ref, tt_ref, key_out, key_in, value_out, value_in, mine_part,
    in_sem, w_sem, rs_send, rs_recv, a_recv, b_recv, x_recv, n_recv, core_recv, sent,
):
    heads = w_ref.shape[0]
    hd = gain_ref.shape[1]
    width = 2 * hd
    rows = vis_ref.shape[0]
    seg = lax.axis_index("segment")
    seq = lax.axis_index("seq")
    ten = lax.axis_index("tensor")
    z, core = seq // 2, seq % 2
    to_x = {"segment": 1 - seg}
    to_core = {"seq": z * 2 + (1 - core)}

    inputs = [
        pltpu.make_async_copy(src, dst, in_sem.at[n])
        for n, (src, dst) in enumerate(
            ((vis_hbm, vis_ref), (gain_hbm, gain_ref), (q_hbm, q_ref), (tt_hbm, tt_ref))
        )
    ]

    def weight_copy(k):
        head = (ten + k) % heads
        cols = pl.ds(pl.multiple_of(head * width, width), width)
        return pltpu.make_async_copy(w_hbm.at[:, cols], w_ref.at[k], w_sem.at[k])

    order = list(range(1, heads)) + [0]
    inputs[0].start()
    for k in order:
        weight_copy(k).start()
    for copy in inputs[1:]:
        copy.start()

    barrier = pltpu.get_barrier_semaphore()
    for k in range(1, heads):
        pl.semaphore_signal(barrier, inc=1, device_id={"tensor": (ten + k) % heads}, device_id_type=MESH)
    near = sorted({d - held for d, held in TREE.items()})
    near = [{"seq": (z + hop) % nz * 2 + core} for jump in near for hop in (jump, nz - jump)]
    for target in near + [to_x, to_core]:
        pl.semaphore_signal(barrier, inc=1, device_id=target, device_id_type=MESH)

    def partial_copy(k, n):
        out, into = ((key_out, key_in), (value_out, value_in))[n]
        return pltpu.make_async_remote_copy(
            src_ref=out.at[k - 1], dst_ref=into.at[k - 1], send_sem=rs_send.at[n], recv_sem=rs_recv.at[n],
            device_id={"tensor": (ten + k) % heads}, device_id_type=MESH,
        )

    inputs[0].wait()
    for k in order:
        weight_copy(k).wait()
        part = jnp.dot(vis_ref[...], w_ref[k], preferred_element_type=F32)
        if k:
            key_out[k - 1] = part[:, :hd].astype(key_out.dtype)
            value_out[k - 1] = part[:, hd:].astype(value_out.dtype)
            if k == 1:
                pl.semaphore_wait(barrier, heads - 1 + len(near) + 2)
            partial_copy(k, 0).start()
            partial_copy(k, 1).start()
        else:
            mine_part[...] = part

    for copy in inputs[1:]:
        copy.wait()
    count = tt_ref.shape[1]
    low_row = tt_ref[0:1, :].astype(F32)
    high_row = tt_ref[1:2, :].astype(F32)
    key_row = jnp.full_like(low_row, float(len(ORDER)))
    for place, (first, last) in enumerate(ORDER):
        key_row = jnp.where((low_row == first) & (high_row == last), float(place), key_row)
    row_id = lax.broadcasted_iota(jnp.int32, (count, count), 0)
    col_id = lax.broadcasted_iota(jnp.int32, (count, count), 1)
    key_col = jnp.sum(jnp.where(row_id == col_id, key_row, 0.0), axis=1, keepdims=True)
    ahead_row = (key_col < key_row) | ((key_col == key_row) & (row_id < col_id))
    place_row = jnp.sum(jnp.where(ahead_row, 1.0, 0.0), axis=0, keepdims=True)
    ahead_col = (key_row < key_col) | ((key_row == key_col) & (col_id < row_id))
    place_col = jnp.sum(jnp.where(ahead_col, 1.0, 0.0), axis=1, keepdims=True)
    perm = row_id.astype(F32) == place_row
    pt_ref[...] = jnp.where(col_id.astype(F32) == place_col, 1.0, 0.0).astype(BF16)
    qs_ref[...] = jnp.dot(
        jnp.where(perm, 1.0, 0.0).astype(BF16), q_ref[...], preferred_element_type=F32
    ).astype(BF16)
    low_sorted = jnp.sum(jnp.where(perm, low_row, 0.0), axis=1, keepdims=True)
    high_sorted = jnp.sum(jnp.where(perm, high_row, 0.0), axis=1, keepdims=True)
    lane = lax.broadcasted_iota(jnp.int32, (count, 128), 1)
    lohi_ref[:, :hd] = jnp.broadcast_to(low_sorted, (count, hd))
    lohi_ref[:, hd:] = jnp.broadcast_to(high_sorted, (count, hd))
    lane_f = lane.astype(F32)
    sees = jnp.where((low_sorted <= lane_f) & (lane_f < high_sorted), 1.0, 0.0)
    for block in range(count // SUB):
        flag_ref[block : block + 1, :] = jnp.max(
            sees[block * SUB : (block + 1) * SUB], axis=0, keepdims=True
        ).astype(jnp.int32)

    def all_of(ref, sem):
        pltpu.make_async_copy(ref, ref, sem).wait()

    all_of(key_in, rs_recv.at[0])
    keys_raw = mine_part[:, :hd]
    for k in range(heads - 1):
        keys_raw = keys_raw + key_in[k].astype(F32)
    mean_sq = jnp.mean(keys_raw * keys_raw, axis=-1, keepdims=True)
    normed = keys_raw * lax.rsqrt(mean_sq + 1e-05) * gain_ref[...]

    def slot(segment, zz, cc):
        return segment * (2 * nz) + zz * 2 + cc

    mine = slot(seg, z, core)
    kv_ref[mine, :, :hd] = normed.astype(BF16)
    all_of(value_in, rs_recv.at[1])
    values_raw = mine_part[:, hd:]
    for k in range(heads - 1):
        values_raw = values_raw + value_in[k].astype(F32)
    kv_ref[mine, :, hd:] = values_raw.astype(BF16)

    sends = [0]

    def move(block, first, size, recv, target):
        piece = kv_ref.at[block, pl.ds(first, size)]
        return pltpu.make_async_remote_copy(
            src_ref=piece, dst_ref=piece, send_sem=sent, recv_sem=recv, device_id=target, device_id_type=MESH
        )

    def go(copy, size):
        sends[0] += size
        copy.start()

    half = nz // 2

    def place(way, d):
        return (z + nz - d) % nz if way == 0 else (z + d) % nz

    def ahead(way, d):
        jump = d - TREE[d]
        hop = jump if way == 0 else nz - jump
        return {"seq": (z + hop) % nz * 2 + core}

    def span_a(way, d):
        return (way * (rows // 2), rows // 2) if d == half else (0, rows)

    def copy_a(way, held, d):
        return move(slot(seg, place(way, held), core), *span_a(way, d), a_recv.at[way, d - 1], ahead(way, d))

    def copy_b(way, held, d):
        return move(slot(1 - seg, place(way, held), core), 0, RING, b_recv.at[way, d - 1], ahead(way, d))

    def comes_b(way, d):
        return d < half or way == 1

    def span_x(way, d):
        first, size = span_a(way, d)
        last = first + size
        first = max(first, RING)
        return first, last - first

    def cross(way, d):
        first, size = span_x(way, d)
        go(move(slot(seg, place(way, d), core), first, size, x_recv.at[way, d], to_x), size)

    def crossed(way, d):
        move(slot(1 - seg, place(way, d), core), *span_x(way, d), x_recv.at[way, d], to_x).wait_recv()

    def swap(side, way, d):
        go(move(slot(side, place(way, d), core), 0, rows, core_recv, to_core), rows)

    def on_a(way, held):
        for d in TREE:
            if TREE[d] == held:
                go(copy_a(way, held, d), span_a(way, d)[1])

    def on_b(way, held):
        for d in TREE:
            if TREE[d] == held and comes_b(way, d):
                go(copy_b(way, held, d), RING)

    both = (0, 1)
    go(move(mine, 0, RING, n_recv, to_x), RING)
    for way in both:
        on_a(way, 0)
    cross(0, 0)
    swap(seg, 0, 0)
    move(slot(1 - seg, z, core), 0, RING, n_recv, to_x).wait_recv()
    for way in both:
        on_b(way, 0)
    waiting = [(0, 0)]

    def take_crossed(keep):
        while len(waiting) > keep:
            way, d = waiting.pop(0)
            crossed(way, d)
            if d < half or way == 1:
                swap(1 - seg, way, d)

    late = []

    def take_b(keep):
        while len(late) > keep:
            d = late.pop(0)
            for way in both:
                if comes_b(way, d):
                    copy_b(way, d, d).wait_recv()
                    on_b(way, d)

    for d in ARRIVAL:
        for way in both:
            copy_a(way, d, d).wait_recv()
            on_a(way, d)
        for way in both:
            cross(way, d)
        late.append(d)
        take_b(BLAG)
        for way in both:
            if d < half or way == 1:
                swap(seg, way, d)
        take_crossed(LAG)
        waiting += [(0, d), (1, d)]
    take_b(0)
    take_crossed(0)

    all_of(kv_ref.at[pl.ds(0, 2 * nz)], core_recv)
    assert sends[0] % rows == 0
    all_of(kv_ref.at[pl.ds(0, sends[0] // rows)], sent)
    all_of(key_out, rs_send.at[0])
    all_of(value_out, rs_send.at[1])


def attend(
    scale, tile_len, least, tokens_ref, flag_ref, kv_ref, qs_ref, pt_ref, lohi_ref, out_ref,
    acc, top, low_sum, sorted_out, s_ref, peak_ref, blocks_of, *, group=4,
):
    tiles = kv_ref.shape[0] // tile_len
    hd = kv_ref.shape[1] // 2
    count = qs_ref.shape[0] // SUB
    heads = qs_ref.shape[1] // hd
    chunk = 256
    acc[...] = jnp.zeros_like(acc)
    low_sum[...] = jnp.zeros_like(low_sum)
    top[...] = jnp.full_like(top, NEG)
    factor = scale * math.log2(math.e)

    def queries_of(picked):
        rows_of = []
        for block in picked:
            src = pl.multiple_of(jnp.where(block == count, 0, block) * SUB, SUB)
            for h in range(heads):
                rows_of.append(qs_ref[pl.ds(src, SUB), h * hd : (h + 1) * hd])
        return jnp.concatenate(rows_of, axis=0)

    def score(tile, c, n_chunks, q, valid):
        at = pl.multiple_of(tile * tile_len + c * chunk, chunk)
        s = lax.dot_general(
            q, kv_ref[pl.ds(at, chunk), :hd], (((1,), (1,)), ((), ())), preferred_element_type=F32
        )
        if c == n_chunks - 1 and c * chunk >= least:
            lane = lax.broadcasted_iota(jnp.int32, s.shape, 1)
            s = jnp.where(lane < valid - c * chunk, s, NEG)
        return s

    def step(tile, n_chunks, picked, following, valid):
        q = None if following is None else queries_of(following)
        peak = peak_ref[...]
        part = summed = best = None
        for c in range(n_chunks):
            cols = slice(c * chunk, (c + 1) * chunk)
            at = pl.multiple_of(tile * tile_len + c * chunk, chunk)
            old = s_ref[:, cols]
            s = None if q is None else score(tile, c, n_chunks, q, valid)
            halves = [
                jnp.exp2((old[:, x : x + hd] - peak) * factor) for x in range(0, chunk, hd)
            ]
            for e in halves:
                part = e if part is None else part + e
            e16 = jnp.concatenate([e.astype(BF16) for e in halves], axis=1)
            o = jnp.dot(e16, kv_ref[pl.ds(at, chunk), hd:], preferred_element_type=F32)
            summed = o if summed is None else summed + o
            if s is not None:
                s_ref[:, cols] = s
                fold = jnp.maximum(s[:, :hd], s[:, hd:])
                best = fold if best is None else jnp.maximum(best, fold)
        high = part.astype(BF16)
        rest = (part - high.astype(F32)).astype(BF16)
        row_sum = jnp.dot(
            jnp.concatenate([high, rest], axis=1), jnp.ones((2 * hd, hd), BF16), preferred_element_type=F32
        )
        merge(tile, picked, peak, row_sum, summed)
        if best is not None:
            peak_ref[...] = jnp.broadcast_to(jnp.max(best, axis=1, keepdims=True), peak_ref.shape)

    def start(tile, n_chunks, picked, valid):
        q = queries_of(picked)
        best = None
        for c in range(n_chunks):
            s = score(tile, c, n_chunks, q, valid)
            s_ref[:, c * chunk : (c + 1) * chunk] = s
            best = s if best is None else jnp.maximum(best, s)
        peak_ref[...] = jnp.broadcast_to(jnp.max(best, axis=1, keepdims=True), peak_ref.shape)

    def merge(tile, picked, peak, row_sum, summed):
        span = heads * SUB
        for i, block in enumerate(picked):
            src = pl.multiple_of(jnp.where(block == count, 0, block) * SUB, SUB)
            low = lohi_ref[pl.ds(src, SUB), :hd]
            high = lohi_ref[pl.ds(src, SUB), hd:]
            tile_f = tile.astype(F32)
            seen = jnp.where((low <= tile_f) & (tile_f < high), 1.0, 0.0)
            seen = jnp.concatenate([seen] * heads, axis=0)
            part_slice = slice(i * span, (i + 1) * span)
            mine = jnp.where(seen > 0.0, peak[part_slice], NEG)
            old = top[block]
            new = jnp.maximum(old, mine)
            keep = jnp.exp2((old - new) * factor)
            take = jnp.where(seen > 0.0, jnp.exp2((mine - new) * factor), 0.0)
            top[block] = new
            low_sum[block] = low_sum[block] * keep + row_sum[part_slice] * take
            acc[block] = acc[block] * keep + summed[part_slice] * take

    def one_tile(tile, carry):
        found = 0
        for block in range(count):
            blocks_of[found] = block
            found = found + flag_ref[block, tile]
        for i in range(2 * group):
            blocks_of[found + i] = count
        trips = (found + group - 1) // group
        valid = tokens_ref[tile]
        base = least // chunk
        extra = (valid - least + chunk - 1) // chunk

        def picked(i):
            return [blocks_of[i * group + j] for j in range(group)]

        for more in range((tile_len - least) // chunk + 1):

            @pl.when((extra == more) & (trips > 0))
            def _(more=more):
                start(tile, base + more, picked(0), valid)

                def pair(i, c):
                    step(tile, base + more, picked(i), picked(i + 1), valid)
                    return c

                lax.fori_loop(0, trips - 1, pair, 0)
                step(tile, base + more, picked(trips - 1), None, valid)

        return carry

    lax.fori_loop(0, tiles, one_tile, 0)

    def close(block, carry):
        src = block * SUB
        low = lohi_ref[pl.ds(src, SUB), :hd]
        high = lohi_ref[pl.ds(src, SUB), hd:]
        unseen = jnp.where(high <= low, 1.0, 0.0)
        unseen = jnp.concatenate([unseen] * heads, axis=0)
        done = (acc[block] / (low_sum[block] + unseen)).astype(BF16)
        for h in range(heads):
            sorted_out[pl.ds(src, SUB), h * hd : (h + 1) * hd] = done[h * SUB : (h + 1) * SUB]
        return carry

    for block in range(count):
        close(block, 0)
    out_ref[...] = jnp.dot(pt_ref[...], sorted_out[...], preferred_element_type=F32).astype(BF16)


def run_attend(tile_tokens, flags, kv, qs, pt, lohi, head_dim):
    text_rows, cols = qs.shape
    tile_len = kv.shape[0] // tile_tokens.shape[0]
    span = (cols // head_dim) * SUB
    blocks = text_rows // SUB
    smem = pl.BlockSpec(memory_space=pltpu.SMEM)
    vmem = pl.BlockSpec(memory_space=pltpu.VMEM)
    return pl.pallas_call(
        functools.partial(attend, head_dim ** (-0.5), tile_len, tile_len // 2),
        out_shape=jax.ShapeDtypeStruct((text_rows, cols), BF16),
        in_specs=[smem, smem, vmem, vmem, vmem, vmem],
        out_specs=vmem,
        scratch_shapes=[
            pltpu.VMEM((blocks + 1, span, head_dim), F32),
            pltpu.VMEM((blocks + 1, span, head_dim), F32),
            pltpu.VMEM((blocks + 1, span, head_dim), F32),
            pltpu.VMEM((text_rows, cols), BF16),
            pltpu.VMEM((4 * span, tile_len), F32),
            pltpu.VMEM((4 * span, head_dim), F32),
            pltpu.SMEM((blocks + 8,), jnp.int32),
        ],
        compiler_params=pltpu.CompilerParams(vmem_limit_bytes=40 << 20),
        name="attend",
    )(tile_tokens, flags, kv, qs, pt, lohi)


def shards(vision_states, kv_weight, key_gain, queries, tile_tokens, text_tiles):
    head_dim = key_gain.shape[0]
    rows = vision_states.shape[0]
    heads = lax.axis_size("tensor")
    nz = lax.axis_size("seq") // 2
    pieces = lax.axis_size("segment") * lax.axis_size("seq")
    depth = vision_states.shape[1]
    text_rows = queries.shape[0]
    q = queries.reshape(text_rows, queries.shape[2])
    vmem = pl.BlockSpec(memory_space=pltpu.VMEM)
    hbm = pl.BlockSpec(memory_space=pltpu.HBM)
    dma = pltpu.SemaphoreType.DMA
    kv, qs, pt, lohi, flags = pl.pallas_call(
        functools.partial(project_gather, nz),
        out_shape=(
            jax.ShapeDtypeStruct((pieces, rows, 2 * head_dim), BF16),
            jax.ShapeDtypeStruct(q.shape, BF16),
            jax.ShapeDtypeStruct((text_rows, text_rows), BF16),
            jax.ShapeDtypeStruct((text_rows, 2 * head_dim), F32),
            jax.ShapeDtypeStruct((text_rows // SUB, 128), jnp.int32),
        ),
        in_specs=[hbm] * 5,
        out_specs=(vmem,) * 5,
        scratch_shapes=[
            pltpu.VMEM((rows, depth), BF16),
            pltpu.VMEM((heads, depth, 2 * head_dim), BF16),
            pltpu.VMEM((1, head_dim), F32),
            pltpu.VMEM(q.shape, BF16),
            pltpu.VMEM((2, text_rows), jnp.int32),
            pltpu.VMEM((heads - 1, rows, head_dim), F32),
            pltpu.VMEM((heads - 1, rows, head_dim), F32),
            pltpu.VMEM((heads - 1, rows, head_dim), VALUE_PART),
            pltpu.VMEM((heads - 1, rows, head_dim), VALUE_PART),
            pltpu.VMEM((rows, 2 * head_dim), F32),
            dma((4,)), dma((heads,)), dma((2,)), dma((2,)),
            dma((2, nz // 2)), dma((2, nz // 2)), dma((2, nz // 2 + 1)), dma, dma, dma,
        ],
        compiler_params=pltpu.CompilerParams(
            collective_id=0, has_side_effects=True, vmem_limit_bytes=40 << 20
        ),
        name="project_gather",
    )(*(pltpu.with_memory_space_constraint(a, pltpu.HBM) for a in (vision_states, kv_weight, key_gain.reshape(1, head_dim), q, text_tiles.T)))
    kv = kv.reshape(pieces * rows, 2 * head_dim)
    out = run_attend(tile_tokens, flags, kv, qs, pt, lohi, head_dim)
    return out.reshape(queries.shape)


def solution(mesh):
    placed = (
        P(("segment", "seq"), "tensor"),
        P("tensor", None),
        P(),
        P("seq", "tensor", "segment"),
        P(),
        P("seq", None),
    )
    return jax.shard_map(
        shards, mesh=mesh, in_specs=placed, out_specs=P("seq", "tensor", "segment"), check_vma=False
    )
```
